128 devices in a mesh: slab: 16 (over x_hi, y, core), head: 8 (over x_lo, z).
Axes of the slice: x: 4 (x_hi: 2, x_lo: 2; x = x_hi * 2 + x_lo), y: 4, z: 4, core: 2. Of those that a mesh axis runs over, the one named last changes fastest.
Arguments:
- section_activations: bfloat16 [448, 384, 256], P('slab'), may hold values from -6 to 6
- kernel_weight: bfloat16 [27, 384, 384], replicated, may hold values from -0.0625 to 0.0625
- packed_output_gradient: bfloat16 [256, 384, 256], P('slab', 'head'), may hold values from -6 to 6
- clip_length: int32 [32], replicated, may hold values from 1 to 27, as said below
- clip_slab_index: int32 [32], replicated, may hold values from 0 to 15, as said below
- packed_clip_order: int32 [32], replicated, may hold values from 0 to 31, each once
Outputs:
- input_grad: bfloat16 [448, 384, 256], P('slab', 'head')
- weight_grad: bfloat16 [27, 384, 384], P(None, 'slab', 'head')
The draws below stay inside these ranges and needn't reach their ends.
Inputs may be any that keep to these rules, and one draw needn't show every extreme that they name: `clip_length`: the lengths of all clips sum to 256. `clip_slab_index`: every slab takes exactly two clips; the frames of a slab lie between 4 and 28, and in every draw one slab holds 28 frames and one holds 4. `packed_clip_order`: each clip appears once.
All inputs are finite; a program needn't handle non-finite values.
Results may differ from the reference program's by a relative error of at most 0.014.
Values may be sent and summed in bfloat16 or wider, within the bound.
A program may use at most 448 MiB of HBM per device.

```python
import math
import jax
import jax.numpy as jnp
from jax import lax

CHANNEL_COUNT = 384
F_SEQ = 16
PIXEL_ROWS = 16
PIXEL_COLUMNS = 16
TAPS = 27
FRAME_PIXELS = 256
SLAB_FRAME_SLOTS = 28
FRAMES_OVERALL = 256
ENC_F = 448
CLIP_COUNT = 32
N_SLAB = 16


def clip_plan(key):
    key = jax.random.fold_in(key, 7)
    key_order, key_delta, key_first, key_place = jax.random.split(key, 4)
    slab_count = CLIP_COUNT // 2
    pair_count = slab_count // 2
    slab_order = jax.random.permutation(key_order, slab_count)
    delta = jax.random.randint(key_delta, (pair_count,), -(F_SEQ // 2), F_SEQ // 2 + 1)
    delta = delta.at[0].set(SLAB_FRAME_SLOTS - F_SEQ)
    loads = jnp.zeros((slab_count,), jnp.int32)
    loads = loads.at[slab_order[0::2]].set(F_SEQ + delta)
    loads = loads.at[slab_order[1::2]].set(F_SEQ - delta)
    first = jax.random.randint(key_first, (slab_count,), 1, loads)
    first = first.at[slab_order[0]].set(1)
    placing = jax.random.permutation(key_place, CLIP_COUNT)
    slab_of = placing // 2
    clip_lengths = jnp.where(placing % 2 == 0, first[slab_of], loads[slab_of] - first[slab_of])
    return (clip_lengths.astype(jnp.int32), slab_of.astype(jnp.int32))


def draw_clip_length(key, part):
    return clip_plan(key)[0]


def draw_clip_slab_index(key, part):
    return clip_plan(key)[1]


def levels(rng, extent, pieces, smallest, largest):
    loudness = 1.0
    for position, shards_of in pieces:
        steps = jax.random.uniform(jax.random.fold_in(jax.random.fold_in(rng, 6), position), (shards_of,), jnp.float32, smallest / len(pieces), largest / len(pieces))
        loudness = loudness * jnp.repeat(jnp.exp(steps), extent[position] // shards_of).reshape((-1,) + (1,) * (len(extent) - 1 - position))
    return loudness


def noise(rng, dims, spread, limit, cuts=(), held_as=jnp.bfloat16):
    level = levels(rng, dims, cuts, -0.22, 0.18) if cuts else 1.0
    array = jax.random.normal(rng, dims, jnp.float32) * spread * level
    return jnp.minimum(jnp.maximum(array, -limit), limit).astype(held_as)


def setup_inputs(seed: int = 0) -> dict:
    arg_keys = jax.random.split(jax.random.key(seed), 7)
    return {
        "section_activations": noise(arg_keys[0], (ENC_F, CHANNEL_COUNT, FRAME_PIXELS), 1.0, 6.0, ((0, 16),)),
        "kernel_weight": noise(arg_keys[1], (TAPS, CHANNEL_COUNT, CHANNEL_COUNT), (TAPS * CHANNEL_COUNT) ** -0.5, 0.0625),
        "packed_output_gradient": noise(arg_keys[2], (FRAMES_OVERALL, CHANNEL_COUNT, FRAME_PIXELS), 1.0, 6.0, ((0, 16), (1, 8))),
        "clip_length": draw_clip_length(jax.random.fold_in(arg_keys[6], 71), 0),
        "clip_slab_index": draw_clip_slab_index(jax.random.fold_in(arg_keys[6], 71), 0),
        "packed_clip_order": jax.random.permutation(arg_keys[5], CLIP_COUNT).astype(jnp.int32),
    }


def slot_lookup(clip_lengths, slabs, order, slab_number, frame_list):
    clip_ids = jnp.arange(clip_lengths.shape[0], dtype=jnp.int32)
    same_slab = slabs[None, :] == slabs[:, None]
    earlier = clip_ids[None, :] < clip_ids[:, None]
    encoder_offset = lax.optimization_barrier(jnp.sum(jnp.where(same_slab & earlier, clip_lengths[None, :], 0), axis=1)).astype(jnp.int32)
    matches = order[None, :] == clip_ids[:, None]
    placing = lax.optimization_barrier(jnp.sum(jnp.where(matches, clip_ids[None, :], 0), axis=1)).astype(jnp.int32)
    prior_frames = placing[None, :] < placing[:, None]
    packed_start = lax.optimization_barrier(jnp.sum(jnp.where(prior_frames, clip_lengths[None, :], 0), axis=1)).astype(jnp.int32)
    slot_list = jnp.arange(frame_list, dtype=jnp.int32)[:, None]
    within_clip = (slabs[None, :] == slab_number) & (slot_list >= encoder_offset[None, :]) & (slot_list < (encoder_offset + clip_lengths)[None, :])
    filled_slots = jnp.any(within_clip, axis=1)
    frame_lag = lax.optimization_barrier(jnp.sum(jnp.where(within_clip, slot_list - encoder_offset[None, :], 0), axis=1)).astype(jnp.int32)
    incoming_sum = lax.optimization_barrier(jnp.sum(jnp.where(within_clip, packed_start[None, :] + slot_list - encoder_offset[None, :], 0), axis=1)).astype(jnp.int32)
    incoming_row = jnp.where(filled_slots, incoming_sum, -1).astype(jnp.int32)
    return (filled_slots, frame_lag, incoming_row)

def pixel_shift(values, row_step, col_step):
    pixels = PIXEL_ROWS * PIXEL_COLUMNS
    margin = PIXEL_COLUMNS + 1
    padded = jnp.pad(values, ((0, 0), (0, 0), (margin, margin)))
    offset = row_step * PIXEL_COLUMNS + col_step
    moved = padded[:, :, margin + offset:margin + offset + pixels]
    positions = jnp.arange(pixels, dtype=jnp.int32)
    pix_row = positions // PIXEL_COLUMNS + row_step
    pix_col = positions % PIXEL_COLUMNS + col_step
    keep = (pix_row >= 0) & (pix_row < PIXEL_ROWS) & (pix_col >= 0) & (pix_col < PIXEL_COLUMNS)
    return jnp.where(keep[None, None, :], moved, jnp.zeros((), values.dtype))

def tap_stack(grads, filled_slots, frame_lag, time_taps):
    stacked = []
    for time_tap in time_taps:
        delay = 2 - time_tap
        keep = filled_slots & (frame_lag >= delay)
        masked = jnp.where(keep[:, None, None], grads, jnp.zeros((), grads.dtype))
        if delay > 0:
            masked = jnp.concatenate([masked[delay:], jnp.zeros((delay,) + masked.shape[1:], masked.dtype)], axis=0)
        for row_tap in range(3):
            for col_tap in range(3):
                stacked.append(pixel_shift(masked, 1 - row_tap, 1 - col_tap))
    return jnp.stack(stacked, axis=1)

def reference(section_activations, kernel_weight, packed_output_gradient, clip_length, clip_slab_index, packed_clip_order):
    slab_inputs = section_activations.reshape(N_SLAB, SLAB_FRAME_SLOTS, CHANNEL_COUNT, FRAME_PIXELS)
    weight_wide = kernel_weight.astype(jnp.float32)
    gradient_scale = 1.0 / math.sqrt(FRAMES_OVERALL * FRAME_PIXELS)

    def per_slab(operands):
        slab_input, slab_number = operands
        filled_slots, frame_lag, incoming_row = slot_lookup(clip_length, clip_slab_index, packed_clip_order, slab_number, SLAB_FRAME_SLOTS)
        frame_rows = jnp.take(packed_output_gradient, jnp.maximum(incoming_row, 0).astype(jnp.int32), axis=0).astype(jnp.float32)
        out_grad = jnp.where(filled_slots[:, None, None], frame_rows, jnp.zeros((), jnp.float32))
        taps = tap_stack(out_grad, filled_slots, frame_lag, (0, 1, 2))
        input_part = jnp.einsum('tio,gtoq->giq', weight_wide, taps, precision=lax.Precision.HIGHEST)
        weight_part = jnp.einsum('giq,gtoq->tio', slab_input.astype(jnp.float32), taps, precision=lax.Precision.HIGHEST)
        return (input_part.astype(jnp.bfloat16), (weight_part * gradient_scale).astype(jnp.bfloat16))
    grads, weights = lax.map(per_slab, (slab_inputs, jnp.arange(N_SLAB, dtype=jnp.int32)))
    input_grad = grads.reshape(ENC_F, CHANNEL_COUNT, FRAME_PIXELS)
    weight_grad = lax.optimization_barrier(jnp.sum(weights.astype(jnp.float32), axis=0)).astype(jnp.bfloat16)
    return (input_grad, weight_grad)
```

```python
import functools
import math

import jax
import jax.numpy as jnp
from jax import lax
from jax.experimental import pallas as pl
from jax.experimental.pallas import tpu as pltpu
from jax.sharding import PartitionSpec as P

MESH = pl.DeviceIdType.MESH
ROWS = 16
COLS = 16
PIX = ROWS * COLS
SLOTS = 28
C = 384
OG = 48
NS = 16
NH = 8
CLS = 8
PER = 5
FD = 4
SCALE = 1.0 / math.sqrt(256 * PIX)


def clip_table(clip_length, clip_slab_index, packed_clip_order):
    ids = jnp.arange(clip_length.shape[0], dtype=jnp.int32)
    place = jnp.sum(
        jnp.where(packed_clip_order[None, :] == ids[:, None], ids[None, :], 0), axis=1
    )
    start = jnp.sum(
        jnp.where(place[None, :] < place[:, None], clip_length[None, :], 0), axis=1
    )
    same = clip_slab_index[None, :] == clip_slab_index[:, None]
    second = jnp.any(same & (ids[None, :] < ids[:, None]), axis=1)
    slabs = jnp.arange(NS, dtype=jnp.int32)[:, None]
    mine = clip_slab_index[None, :] == slabs
    vals = jnp.stack([start, clip_length])[None, None]
    pick = jnp.stack([mine & ~second[None, :], mine & second[None, :]], axis=1)
    return jnp.sum(jnp.where(pick[:, :, None, :], vals, 0), axis=3).reshape(-1)


def shifts(x, lane):
    row, col = lane // COLS, lane % COLS
    out = []
    for a in range(3):
        for b in range(3):
            dr, dc = 1 - a, 1 - b
            off = dr * COLS + dc
            if off == 0:
                out.append(x)
                continue
            moved = pltpu.roll(x, (-off) % PIX, 1)
            ok = (row + dr >= 0) & (row + dr < ROWS) & (col + dc >= 0) & (col + dc < COLS)
            out.append(jnp.where(ok, moved, jnp.zeros_like(moved)))
    return out


def body(
    tab, g, act, w, dx, dw,
    act_v, w_v, rbuf, qbuf, dbuf, gs, taps, part, psend, precv, ebuf, hbuf, osend, xbuf,
    s1, r1, s2, r2, s3, r3, s4, r4, s5, r5, la, lw, lo,
):
    ms = lax.axis_index("slab")
    mh = lax.axis_index("head")

    loads = []
    for f in range(SLOTS):
        loads.append(pltpu.make_async_copy(
            act.at[f], act_v.at[:, pl.ds(f * PIX, PIX)], la.at[f]))
    wloads = []
    for t in range(27):
        wloads.append(pltpu.make_async_copy(
            w.at[t], w_v.at[t // 9, :, pl.ds((t % 9) * C, C)], lw.at[t]))
    for cp in loads + wloads:
        cp.start()

    barrier = pltpu.get_barrier_semaphore()
    for k in range(1, NS):
        pl.semaphore_signal(barrier, inc=1, device_id={"slab": (ms + k) % NS}, device_id_type=MESH)
    for k in range(1, NH):
        pl.semaphore_signal(barrier, inc=1, device_id={"head": (mh + k) % NH}, device_id_type=MESH)
    pl.semaphore_wait(barrier, NS - 1 + NH - 1)

    def piece(d):
        return g.at[:, d // 2, :, pl.ds(pl.multiple_of((d % 2) * 128, 128), 128)]

    own = pltpu.make_async_copy(piece(ms), rbuf.at[ms], lo.at[0])
    own.start()
    first = []
    for k in range(1, NS):
        d = (ms + k) % NS
        cp = pltpu.make_async_remote_copy(
            src_ref=piece(d), dst_ref=rbuf.at[ms], send_sem=s1.at[k], recv_sem=r1.at[k],
            device_id={"slab": d}, device_id_type=MESH)
        cp.start()
        first.append(cp)
    own.wait()
    for cp in first:
        cp.wait()

    cls = ms // 2
    half = pl.ds(pl.multiple_of((ms % 2) * 128, 128), 128)
    second = []
    for k in list(range(1, NS)) + [0]:
        d = (ms + k) % NS
        p1, l1, p2 = tab[d * 4], tab[d * 4 + 1], tab[d * 4 + 2]
        o1 = (cls - p1 + 256) % CLS
        o2 = (cls - p2 + 256) % CLS
        n1 = (l1 - o1 + 7) // CLS
        for j in range(PER):
            i1 = (p1 + o1) // CLS + j
            i2 = (p2 + o2) // CLS + j - n1
            idx = jnp.where(j < n1, i1, i2)
            idx = jnp.minimum(jnp.maximum(idx, 0), 31)
            qbuf[d, j] = rbuf[idx // 2, idx % 2]
        if k:
            cp = pltpu.make_async_remote_copy(
                src_ref=qbuf.at[d], dst_ref=dbuf.at[cls, :, :, half],
                send_sem=s2.at[k], recv_sem=r2.at[k],
                device_id={"slab": d}, device_id_type=MESH)
            cp.start()
            second.append(cp)
        else:
            own = pltpu.make_async_copy(qbuf.at[d], dbuf.at[cls, :, :, half], lo.at[0])
            own.start()
            own.wait()
    for cp in second:
        cp.wait()

    p1, l1, p2, l2 = tab[ms * 4], tab[ms * 4 + 1], tab[ms * 4 + 2], tab[ms * 4 + 3]

    def age(j):
        return jnp.where(j < l1, j, j - l1)

    def place(j, _):
        one = j < l1
        p = jnp.where(one, p1 + j, p2 + j - l1)
        c = p % CLS
        n1 = (l1 - (c - p1 + 256) % CLS + 7) // CLS
        r = jnp.where(one, j // CLS, n1 + (j - l1) // CLS)
        live = j < l1 + l2
        c = jnp.where(live, c, 0)
        r = jnp.where(live, r, 0)
        x = dbuf[c, r]
        gs[j] = jnp.where(live, x, jnp.zeros_like(x))
        return 0

    lax.fori_loop(0, SLOTS, place, 0)
    for j in range(SLOTS, SLOTS + FD + 2):
        gs[j] = jnp.zeros((OG, PIX), jnp.bfloat16)

    third = []
    for k in range(1, NH):
        h = (mh + k) % NH
        cp = pltpu.make_async_remote_copy(
            src_ref=gs.at[pl.ds(h * FD, FD + 2)],
            dst_ref=ebuf.at[:, pl.ds(pl.multiple_of(mh * OG, OG), OG), :],
            send_sem=s3.at[k], recv_sem=r3.at[k],
            device_id={"head": h}, device_id_type=MESH)
        cp.start()
        third.append(cp)
    own = pltpu.make_async_copy(
        gs.at[pl.ds(mh * FD, FD + 2)],
        ebuf.at[:, pl.ds(pl.multiple_of(mh * OG, OG), OG), :], lo.at[0])
    own.start()

    lane48 = lax.broadcasted_iota(jnp.int32, (OG, PIX), 1)

    def build(f, _):
        x = gs[f]
        sh = shifts(x, lane48)
        for d in range(3):
            keep = age(f) >= d
            at = pl.ds(pl.multiple_of((f - d + 2) * PIX, PIX), PIX)
            for ab in range(9):
                v = sh[ab]
                if d:
                    v = jnp.where(keep, v, jnp.zeros_like(v))
                taps[(9 * (2 - d) + ab) * OG:(9 * (2 - d) + ab + 1) * OG, at] = v
        return 0

    lax.fori_loop(0, SLOTS + 2, build, 0)
    for cp in loads:
        cp.wait()
    part[...] = jnp.zeros_like(part)

    def mul(n, _):
        a4 = act_v[:, pl.ds(pl.multiple_of(n * 4 * PIX, 4 * PIX), 4 * PIX)]
        b4 = taps[:, pl.ds(pl.multiple_of((n * 4 + 2) * PIX, 2 * PIX), 4 * PIX)]
        part[...] += lax.dot_general(
            a4, b4, (((1,), (1,)), ((), ())), preferred_element_type=jnp.float32)
        return 0

    lax.fori_loop(0, SLOTS // 4, mul, 0)

    fourth = []
    for k in list(range(1, NS)) + [0]:
        d = (ms + k) % NS
        psend[d] = (part[pl.ds(pl.multiple_of(d * 24, 8), 24), :] * SCALE).astype(jnp.bfloat16)
        if k:
            cp = pltpu.make_async_remote_copy(
                src_ref=psend.at[d], dst_ref=precv.at[ms],
                send_sem=s4.at[k], recv_sem=r4.at[k],
                device_id={"slab": d}, device_id_type=MESH)
            cp.start()
            fourth.append(cp)
    precv[ms] = psend[ms]

    own.wait()
    for cp in third:
        cp.wait()
    for cp in wloads:
        cp.wait()
    lane384 = lax.broadcasted_iota(jnp.int32, (C, PIX), 1)

    def hbuild(f, _):
        sh = shifts(ebuf[f], lane384)
        at = pl.ds(pl.multiple_of(f * PIX, PIX), PIX)
        for ab in range(9):
            hbuf[ab * C:(ab + 1) * C, at] = sh[ab]
        return 0

    lax.fori_loop(0, FD + 2, hbuild, 0)

    def grad(f, _):
        total = jnp.zeros((C, PIX), jnp.float32)
        for d in range(3):
            at = pl.ds(pl.multiple_of((f + d) * PIX, PIX), PIX)
            y = jnp.dot(w_v[2 - d], hbuf[:, at], preferred_element_type=jnp.float32)
            if d:
                y = jnp.where(age(mh * FD + f + d) >= d, y, 0.0)
            total += y
        total = total.astype(jnp.bfloat16)
        for h in range(NH):
            osend[f, h] = total[h * OG:(h + 1) * OG]
        return 0

    fifth = []

    @pl.when(mh < SLOTS // FD)
    def _():
        lax.fori_loop(0, FD, grad, 0)
        xbuf[pl.ds(mh * FD, FD)] = osend[:, mh]
        for k in range(1, NH):
            h = (mh + k) % NH
            pltpu.make_async_remote_copy(
                src_ref=osend.at[:, h], dst_ref=xbuf.at[pl.ds(mh * FD, FD)],
                send_sem=s5.at[k], recv_sem=r5.at[k],
                device_id={"head": h}, device_id_type=MESH).start()

    for cp in fourth:
        cp.wait()
    acc = precv[0].astype(jnp.float32)
    for s in range(1, NS):
        acc += precv[s].astype(jnp.float32)
    dw[...] = acc.astype(jnp.bfloat16)

    for k in range(1, NH):
        src = (mh - k + NH) % NH
        h = (mh + k) % NH

        def out_copy():
            return pltpu.make_async_remote_copy(
                src_ref=osend.at[:, h], dst_ref=xbuf.at[pl.ds(mh * FD, FD)],
                send_sem=s5.at[k], recv_sem=r5.at[k],
                device_id={"head": h}, device_id_type=MESH)

        @pl.when(mh < SLOTS // FD)
        def _():
            out_copy().wait_send()

        @pl.when(src < SLOTS // FD)
        def _():
            out_copy().wait_recv()

    dx[...] = xbuf[pl.ds(0, SLOTS)]


def shards(act, w, g, clip_length, clip_slab_index, packed_clip_order):
    tab = clip_table(clip_length, clip_slab_index, packed_clip_order)
    bf = jnp.bfloat16
    dma = pltpu.SemaphoreType.DMA
    anyspace = pl.BlockSpec(memory_space=pl.ANY)
    vmem = pl.BlockSpec(memory_space=pltpu.VMEM)
    dx, dw = pl.pallas_call(
        body,
        out_shape=(
            jax.ShapeDtypeStruct((SLOTS, OG, PIX), bf),
            jax.ShapeDtypeStruct((24, 27 * OG), bf),
        ),
        in_specs=[pl.BlockSpec(memory_space=pltpu.SMEM), anyspace, anyspace, anyspace],
        out_specs=(vmem, vmem),
        scratch_shapes=[
            pltpu.VMEM((C, SLOTS * PIX), bf),
            pltpu.VMEM((3, C, 9 * C), bf),
            pltpu.VMEM((NS, 2, OG, 128), bf),
            pltpu.VMEM((NS, PER, OG, 128), bf),
            pltpu.VMEM((CLS, PER, OG, PIX), bf),
            pltpu.VMEM((SLOTS + FD + 2, OG, PIX), bf),
            pltpu.VMEM((27 * OG, (SLOTS + 4) * PIX), bf),
            pltpu.VMEM((C, 27 * OG), jnp.float32),
            pltpu.VMEM((NS, 24, 27 * OG), bf),
            pltpu.VMEM((NS, 24, 27 * OG), bf),
            pltpu.VMEM((FD + 2, C, PIX), bf),
            pltpu.VMEM((9 * C, (FD + 2) * PIX), bf),
            pltpu.VMEM((FD, NH, OG, PIX), bf),
            pltpu.VMEM((NH * FD, OG, PIX), bf),
            dma((NS,)), dma((NS,)), dma((NS,)), dma((NS,)), dma((NH,)), dma((NH,)),
            dma((NS,)), dma((NS,)), dma((NH,)), dma((NH,)),
            dma((SLOTS,)), dma((27,)), dma((1,)),
        ],
        compiler_params=pltpu.CompilerParams(
            collective_id=0, has_side_effects=True, vmem_limit_bytes=67043328),
    )(tab, g.reshape(2, 8, OG, PIX), act, w)
    return dx, dw.reshape(24, 27, OG).transpose(1, 0, 2)


def solution(mesh):
    return jax.shard_map(
        shards,
        mesh=mesh,
        in_specs=(P("slab", None, None), P(), P("slab", "head", None), P(), P(), P()),
        out_specs=(P("slab", "head", None), P(None, "slab", "head")),
        check_vma=False,
    )
```

```python
import functools
import math

import jax
import jax.numpy as jnp
from jax import lax
from jax.experimental import pallas as pl
from jax.experimental.pallas import tpu as pltpu
from jax.sharding import PartitionSpec as P

MESH = pl.DeviceIdType.MESH
ROWS = 16
COLS = 16
PIX = ROWS * COLS
SLOTS = 28
C = 384
OG = 48
NS = 16
NH = 8
CLS = 8
PER = 5
FD = 4
NC = 3
CH = OG // NC
CLIPS = 32
SCALE = 1.0 / math.sqrt(256 * PIX)


def clip_table(length, slab, order, pk, tab):
    def walk(k, at):
        c = order[k]
        n = length[c]
        pk[0, k] = slab[c]
        pk[1, k] = n
        pk[2, k] = at
        return at + n

    lax.fori_loop(0, CLIPS, walk, 0)

    def row(d, _):
        ka, kb = jnp.int32(0), jnp.int32(0)
        for k in range(CLIPS):
            hit = pk[0, k] == d
            kb = jnp.where(hit, ka, kb)
            ka = jnp.where(hit, k, ka)
        swap = order[ka] > order[kb]
        k1 = jnp.where(swap, kb, ka)
        k2 = jnp.where(swap, ka, kb)
        tab[d * 4] = pk[2, k1]
        tab[d * 4 + 1] = pk[1, k1]
        tab[d * 4 + 2] = pk[2, k2]
        tab[d * 4 + 3] = pk[1, k2]
        return 0

    lax.fori_loop(0, NS, row, 0)


def shifts(x, lane):
    row, col = lane // COLS, lane % COLS
    out = []
    for a in range(3):
        for b in range(3):
            dr, dc = 1 - a, 1 - b
            off = dr * COLS + dc
            if off == 0:
                out.append(x)
                continue
            moved = pltpu.roll(x, (-off) % PIX, 1)
            ok = (row + dr >= 0) & (row + dr < ROWS) & (col + dc >= 0) & (col + dc < COLS)
            out.append(jnp.where(ok, moved, jnp.zeros_like(moved)))
    return out


def body(
    length, slab, order, g, act, w, dx, dw,
    pk, tab, pick, act_v, w_v, rbuf0, rbuf1, rbuf2, qbuf, dbuf0, dbuf1, dbuf2, gs, taps, part, psend, precv, ebuf, hbuf, osend, xbuf,
    s1, r1, s2, r2, s3, r3, s4, r4, s5, r5, la, lw, lo,
):
    ms = lax.axis_index("slab")
    mh = lax.axis_index("head")

    loads = []
    for f in range(SLOTS):
        loads.append(pltpu.make_async_copy(
            act.at[f], act_v.at[:, pl.ds(f * PIX, PIX)], la.at[f]))
    wloads = []
    for t in range(27):
        wloads.append(pltpu.make_async_copy(
            w.at[t], w_v.at[t // 9, :, pl.ds((t % 9) * C, C)], lw.at[t]))
    for cp in loads + wloads:
        cp.start()

    barrier = pltpu.get_barrier_semaphore()
    for k in range(1, NS):
        pl.semaphore_signal(barrier, inc=1, device_id={"slab": (ms + k) % NS}, device_id_type=MESH)
    for k in range(1, NH):
        pl.semaphore_signal(barrier, inc=1, device_id={"head": (mh + k) % NH}, device_id_type=MESH)
    pl.semaphore_wait(barrier, NS - 1 + NH - 1)

    def piece(d, cs):
        return g.at[:, d // 2, cs, pl.ds(pl.multiple_of((d % 2) * 128, 128), 128)]

    rbuf, dbuf = (rbuf0, rbuf1, rbuf2), (dbuf0, dbuf1, dbuf2)
    chunks = [pl.ds(c * CH, CH) for c in range(NC)]
    own = []
    for c in range(NC):
        cp = pltpu.make_async_copy(piece(ms, chunks[c]), rbuf[c].at[ms], lo.at[c])
        cp.start()
        own.append(cp)
    first = []
    for c in range(NC):
        for k in range(1, NS):
            d = (ms + k) % NS
            cp = pltpu.make_async_remote_copy(
                src_ref=piece(d, chunks[c]), dst_ref=rbuf[c].at[ms],
                send_sem=s1.at[c, k], recv_sem=r1.at[c, k],
                device_id={"slab": d}, device_id_type=MESH)
            cp.start()
            first.append(cp)

    clip_table(length, slab, order, pk, tab)
    cls = ms // 2
    half = pl.ds(pl.multiple_of((ms % 2) * 128, 128), 128)

    def choose(d, _):
        p1, l1, p2 = tab[d * 4], tab[d * 4 + 1], tab[d * 4 + 2]
        o1 = (cls - p1 + 256) % CLS
        o2 = (cls - p2 + 256) % CLS
        n1 = (l1 - o1 + 7) // CLS
        for j in range(PER):
            i1 = (p1 + o1) // CLS + j
            i2 = (p2 + o2) // CLS + j - n1
            idx = jnp.where(j < n1, i1, i2)
            pick[d * PER + j] = jnp.minimum(jnp.maximum(idx, 0), 31)
        return 0

    lax.fori_loop(0, NS, choose, 0)
    for cp in own:
        cp.wait()
    second = []
    for c in range(NC):
        for cp in first[c * (NS - 1):(c + 1) * (NS - 1)]:
            cp.wait_recv()
        for k in list(range(1, NS)) + [0]:
            d = (ms + k) % NS
            for j in range(PER):
                idx = pick[d * PER + j]
                qbuf[d, j, c * CH:(c + 1) * CH] = rbuf[c][idx // 2, idx % 2]
            if k:
                cp = pltpu.make_async_remote_copy(
                    src_ref=qbuf.at[d, :, chunks[c], :],
                    dst_ref=dbuf[c].at[cls, :, :, half],
                    send_sem=s2.at[c, k], recv_sem=r2.at[c, k],
                    device_id={"slab": d}, device_id_type=MESH)
                cp.start()
                second.append(cp)
    own = []
    for c in range(NC):
        cp = pltpu.make_async_copy(
            qbuf.at[ms, :, chunks[c], :], dbuf[c].at[cls, :, :, half], lo.at[c])
        cp.start()
        own.append(cp)
    for cp in own:
        cp.wait()

    p1, l1, p2, l2 = tab[ms * 4], tab[ms * 4 + 1], tab[ms * 4 + 2], tab[ms * 4 + 3]

    def age(j):
        return jnp.where(j < l1, j, j - l1)

    low = mh < SLOTS // FD
    lane = lax.broadcasted_iota(jnp.int32, (CH, PIX), 1)
    third = []
    for c in range(NC):
        cs = slice(c * CH, (c + 1) * CH)
        for cp in second[c * (NS - 1):(c + 1) * (NS - 1)]:
            cp.wait_recv()

        def place(j, _):
            one = j < l1
            p = jnp.where(one, p1 + j, p2 + j - l1)
            q = p % CLS
            n1 = (l1 - (q - p1 + 256) % CLS + 7) // CLS
            r = jnp.where(one, j // CLS, n1 + (j - l1) // CLS)
            live = j < l1 + l2
            q = jnp.where(live, q, 0)
            r = jnp.where(live, r, 0)
            x = dbuf[c][q, r]
            gs[j, cs] = jnp.where(live, x, jnp.zeros_like(x))
            return 0

        lax.fori_loop(0, SLOTS, place, 0)
        if c == 0:
            for j in range(SLOTS, SLOTS + FD + 2):
                gs[j] = jnp.zeros((OG, PIX), jnp.bfloat16)

        for k in range(1, NH):
            h = (mh + k) % NH
            cp = pltpu.make_async_remote_copy(
                src_ref=gs.at[pl.ds(h * FD, FD + 2), chunks[c], :],
                dst_ref=ebuf.at[:, pl.ds(pl.multiple_of(mh * OG + c * CH, CH), CH), :],
                send_sem=s3.at[c, k], recv_sem=r3.at[c, k],
                device_id={"head": h}, device_id_type=MESH)
            third.append((h, cp))

            @pl.when(h < SLOTS // FD)
            def _(cp=cp):
                cp.start()

        def build(f, _):
            x = gs[f, cs]
            sh = shifts(x, lane)
            for d in range(3):
                keep = age(f) >= d
                at = pl.ds(pl.multiple_of((f - d + 2) * PIX, PIX), PIX)
                for ab in range(9):
                    v = sh[ab]
                    if d:
                        v = jnp.where(keep, v, jnp.zeros_like(v))
                    t = 9 * (2 - d) + ab
                    taps[(c * 27 + t) * CH:(c * 27 + t + 1) * CH, at] = v
            return 0

        lax.fori_loop(0, SLOTS + 2, build, 0, unroll=5)
    own3 = pltpu.make_async_copy(
        gs.at[pl.ds(mh * FD, FD + 2)],
        ebuf.at[:, pl.ds(pl.multiple_of(mh * OG, OG), OG), :], lo.at[0])
    own3.start()

    for cp in loads:
        cp.wait()
    part[...] = jnp.zeros_like(part)

    def mul(n, _):
        a4 = act_v[:, pl.ds(pl.multiple_of(n * 4 * PIX, 4 * PIX), 4 * PIX)]
        b4 = taps[:, pl.ds(pl.multiple_of((n * 4 + 2) * PIX, 2 * PIX), 4 * PIX)]
        part[...] += lax.dot_general(
            a4, b4, (((1,), (1,)), ((), ())), preferred_element_type=jnp.float32)
        return 0

    lax.fori_loop(0, SLOTS // 4, mul, 0)

    fourth = []
    for k in list(range(1, NS)) + [0]:
        d = (ms + k) % NS
        psend[d] = (part[pl.ds(pl.multiple_of(d * 24, 8), 24), :] * SCALE).astype(jnp.bfloat16)
        if k:
            cp = pltpu.make_async_remote_copy(
                src_ref=psend.at[d], dst_ref=precv.at[ms],
                send_sem=s4.at[k], recv_sem=r4.at[k],
                device_id={"slab": d}, device_id_type=MESH)
            cp.start()
            fourth.append(cp)
    precv[ms] = psend[ms]

    own3.wait()
    for cp in wloads:
        cp.wait()
    lane384 = lax.broadcasted_iota(jnp.int32, (C, PIX), 1)

    def hbuild(f, _):
        sh = shifts(ebuf[f], lane384)
        at = pl.ds(pl.multiple_of(f * PIX, PIX), PIX)
        for ab in range(9):
            hbuf[ab * C:(ab + 1) * C, at] = sh[ab]
        return 0

    def grad(f, _):
        total = jnp.zeros((C, PIX), jnp.float32)
        for d in range(3):
            at = pl.ds(pl.multiple_of((f + d) * PIX, PIX), PIX)
            y = jnp.dot(w_v[2 - d], hbuf[:, at], preferred_element_type=jnp.float32)
            if d:
                y = jnp.where(age(mh * FD + f + d) >= d, y, 0.0)
            total += y
        total = total.astype(jnp.bfloat16)
        for h in range(NH):
            osend[f, h] = total[h * OG:(h + 1) * OG]
        for k in range(1, NH):
            out_copy(k, f).start()
        return 0

    def out_copy(k, f):
        h = (mh + k) % NH
        return pltpu.make_async_remote_copy(
            src_ref=osend.at[f, h], dst_ref=xbuf.at[mh * FD + f],
            send_sem=s5.at[k, f], recv_sem=r5.at[k, f],
            device_id={"head": h}, device_id_type=MESH)

    @pl.when(low)
    def _():
        for _, cp in third:
            cp.wait_recv()
        lax.fori_loop(0, FD + 2, hbuild, 0)
        lax.fori_loop(0, FD, grad, 0)
        xbuf[pl.ds(mh * FD, FD)] = osend[:, mh]

    for cp in fourth:
        cp.wait()
    acc = precv[0].astype(jnp.float32)
    for s in range(1, NS):
        acc += precv[s].astype(jnp.float32)
    acc = acc.astype(jnp.bfloat16)
    for c in range(NC):
        for t in range(27):
            dw[t, :, c * CH:(c + 1) * CH] = acc[:, (c * 27 + t) * CH:(c * 27 + t + 1) * CH]

    for cp in first + second:
        cp.wait_send()
    for h, cp in third:
        @pl.when(h < SLOTS // FD)
        def _(cp=cp):
            cp.wait_send()

    @pl.when(low)
    def _():
        for k in range(1, NH):
            for f in range(FD):
                out_copy(k, f).wait_send()

    for k in range(1, NH):
        @pl.when((mh - k + NH) % NH < SLOTS // FD)
        def _(k=k):
            for f in range(FD):
                out_copy(k, f).wait_recv()

    dx[...] = xbuf[pl.ds(0, SLOTS)]


def shards(act, w, g, clip_length, clip_slab_index, packed_clip_order):
    bf = jnp.bfloat16
    dma = pltpu.SemaphoreType.DMA
    anyspace = pl.BlockSpec(memory_space=pl.ANY)
    vmem = pl.BlockSpec(memory_space=pltpu.VMEM)
    dx, dw = pl.pallas_call(
        body,
        out_shape=(
            jax.ShapeDtypeStruct((SLOTS, OG, PIX), bf),
            jax.ShapeDtypeStruct((27, 24, OG), bf),
        ),
        in_specs=[pl.BlockSpec(memory_space=pltpu.SMEM)] * 3 + [anyspace, anyspace, anyspace],
        out_specs=(vmem, vmem),
        scratch_shapes=[
            pltpu.SMEM((3, CLIPS), jnp.int32),
            pltpu.SMEM((NS * 4,), jnp.int32),
            pltpu.SMEM((NS * PER,), jnp.int32),
            pltpu.VMEM((C, SLOTS * PIX), bf),
            pltpu.VMEM((3, C, 9 * C), bf),
            *[pltpu.VMEM((NS, 2, CH, 128), bf) for _ in range(NC)],
            pltpu.VMEM((NS, PER, OG, 128), bf),
            *[pltpu.VMEM((CLS, PER, CH, PIX), bf) for _ in range(NC)],
            pltpu.VMEM((SLOTS + FD + 2, OG, PIX), bf),
            pltpu.VMEM((27 * OG, (SLOTS + 4) * PIX), bf),
            pltpu.VMEM((C, 27 * OG), jnp.float32),
            pltpu.VMEM((NS, 24, 27 * OG), bf),
            pltpu.VMEM((NS, 24, 27 * OG), bf),
            pltpu.VMEM((FD + 2, C, PIX), bf),
            pltpu.VMEM((9 * C, (FD + 2) * PIX), bf),
            pltpu.VMEM((FD, NH, OG, PIX), bf),
            pltpu.VMEM((NH * FD, OG, PIX), bf),
            dma((NC, NS)), dma((NC, NS)), dma((NC, NS)), dma((NC, NS)),
            dma((NC, NH)), dma((NC, NH)), dma((NS,)), dma((NS,)),
            dma((NH, FD)), dma((NH, FD)),
            dma((SLOTS,)), dma((27,)), dma((NC,)),
        ],
        compiler_params=pltpu.CompilerParams(
            collective_id=0, has_side_effects=True, vmem_limit_bytes=67043328),
    )(clip_length, clip_slab_index, packed_clip_order, g.reshape(2, 8, OG, PIX), act, w)
    return dx, dw


def solution(mesh):
    return jax.shard_map(
        shards,
        mesh=mesh,
        in_specs=(P("slab", None, None), P(), P("slab", "head", None), P(), P(), P()),
        out_specs=(P("slab", "head", None), P(None, "slab", "head")),
        check_vma=False,
    )
```

```python
import functools
import math

import jax
import jax.numpy as jnp
from jax import lax
from jax.experimental import pallas as pl
from jax.experimental.pallas import tpu as pltpu
from jax.sharding import PartitionSpec as P

MESH = pl.DeviceIdType.MESH
ROWS = 16
COLS = 16
PIX = ROWS * COLS
SLOTS = 28
C = 384
OG = 48
NS = 16
NH = 8
CLS = 8
PER = 5
FD = 4
NC = 3
CH = OG // NC
CLIPS = 32
CUTS = ((0, 768), (768, 27 * OG))
SCALE = 1.0 / math.sqrt(256 * PIX)


def clip_table(length, slab, order, pk, tab):
    def walk(k, at):
        c = order[k]
        n = length[c]
        pk[0, k] = slab[c]
        pk[1, k] = n
        pk[2, k] = at
        return at + n

    lax.fori_loop(0, CLIPS, walk, 0)

    def row(d, _):
        ka, kb = jnp.int32(0), jnp.int32(0)
        for k in range(CLIPS):
            hit = pk[0, k] == d
            kb = jnp.where(hit, ka, kb)
            ka = jnp.where(hit, k, ka)
        swap = order[ka] > order[kb]
        k1 = jnp.where(swap, kb, ka)
        k2 = jnp.where(swap, ka, kb)
        tab[d * 4] = pk[2, k1]
        tab[d * 4 + 1] = pk[1, k1]
        tab[d * 4 + 2] = pk[2, k2]
        tab[d * 4 + 3] = pk[1, k2]
        return 0

    lax.fori_loop(0, NS, row, 0)


def shifts(x, lane):
    row, col = lane // COLS, lane % COLS
    out = []
    for a in range(3):
        for b in range(3):
            dr, dc = 1 - a, 1 - b
            off = dr * COLS + dc
            if off == 0:
                out.append(x)
                continue
            moved = pltpu.roll(x, (-off) % PIX, 1)
            ok = (row + dr >= 0) & (row + dr < ROWS) & (col + dc >= 0) & (col + dc < COLS)
            out.append(jnp.where(ok, moved, jnp.zeros_like(moved)))
    return out


def body(
    length, slab, order, g, act, w, dx, dw,
    pk, tab, pick, act_v, w_v, rbuf0, rbuf1, rbuf2, qbuf, dbuf0, dbuf1, dbuf2, gs, taps, part, psend0, psend1, precv0, precv1, ebuf, hbuf, osend, xbuf,
    s1, r1, s2, r2, s3, r3, s4, r4, s5, r5, la, lw, lo,
):
    ms = lax.axis_index("slab")
    mh = lax.axis_index("head")

    loads = []
    for f in range(SLOTS):
        loads.append(pltpu.make_async_copy(
            act.at[f], act_v.at[:, pl.ds(f * PIX, PIX)], la.at[f]))
    wloads = []
    for t in range(27):
        wloads.append(pltpu.make_async_copy(
            w.at[t], w_v.at[t // 9, :, pl.ds((t % 9) * C, C)], lw.at[t]))
    for cp in loads + wloads:
        cp.start()

    barrier = pltpu.get_barrier_semaphore()
    for k in range(1, NS):
        pl.semaphore_signal(barrier, inc=1, device_id={"slab": (ms + k) % NS}, device_id_type=MESH)
    for k in range(1, NH):
        pl.semaphore_signal(barrier, inc=1, device_id={"head": (mh + k) % NH}, device_id_type=MESH)
    pl.semaphore_wait(barrier, NS - 1 + NH - 1)

    def piece(d, cs):
        return g.at[:, d // 2, cs, pl.ds(pl.multiple_of((d % 2) * 128, 128), 128)]

    psend, precv = (psend0, psend1), (precv0, precv1)
    rbuf, dbuf = (rbuf0, rbuf1, rbuf2), (dbuf0, dbuf1, dbuf2)
    chunks = [pl.ds(c * CH, CH) for c in range(NC)]
    own = []
    for c in range(NC):
        cp = pltpu.make_async_copy(piece(ms, chunks[c]), rbuf[c].at[ms], lo.at[c])
        cp.start()
        own.append(cp)
    first = []
    for c in range(NC):
        for k in range(1, NS):
            d = (ms + k) % NS
            cp = pltpu.make_async_remote_copy(
                src_ref=piece(d, chunks[c]), dst_ref=rbuf[c].at[ms],
                send_sem=s1.at[c, k], recv_sem=r1.at[c, k],
                device_id={"slab": d}, device_id_type=MESH)
            cp.start()
            first.append(cp)

    clip_table(length, slab, order, pk, tab)
    cls = ms // 2
    half = pl.ds(pl.multiple_of((ms % 2) * 128, 128), 128)

    def choose(d, _):
        p1, l1, p2 = tab[d * 4], tab[d * 4 + 1], tab[d * 4 + 2]
        o1 = (cls - p1 + 256) % CLS
        o2 = (cls - p2 + 256) % CLS
        n1 = (l1 - o1 + 7) // CLS
        for j in range(PER):
            i1 = (p1 + o1) // CLS + j
            i2 = (p2 + o2) // CLS + j - n1
            idx = jnp.where(j < n1, i1, i2)
            pick[d * PER + j] = jnp.minimum(jnp.maximum(idx, 0), 31)
        return 0

    lax.fori_loop(0, NS, choose, 0)
    for cp in own:
        cp.wait()
    second = []
    for c in range(NC):
        for cp in first[c * (NS - 1):(c + 1) * (NS - 1)]:
            cp.wait_recv()
        for k in list(range(1, NS)) + [0]:
            d = (ms + k) % NS
            for j in range(PER):
                idx = pick[d * PER + j]
                qbuf[d, j, c * CH:(c + 1) * CH] = rbuf[c][idx // 2, idx % 2]
            if k:
                cp = pltpu.make_async_remote_copy(
                    src_ref=qbuf.at[d, :, chunks[c], :],
                    dst_ref=dbuf[c].at[cls, :, :, half],
                    send_sem=s2.at[c, k], recv_sem=r2.at[c, k],
                    device_id={"slab": d}, device_id_type=MESH)
                cp.start()
                second.append(cp)
    own = []
    for c in range(NC):
        cp = pltpu.make_async_copy(
            qbuf.at[ms, :, chunks[c], :], dbuf[c].at[cls, :, :, half], lo.at[c])
        cp.start()
        own.append(cp)
    for cp in own:
        cp.wait()

    p1, l1, p2, l2 = tab[ms * 4], tab[ms * 4 + 1], tab[ms * 4 + 2], tab[ms * 4 + 3]

    def age(j):
        return jnp.where(j < l1, j, j - l1)

    low = mh < SLOTS // FD
    lane = lax.broadcasted_iota(jnp.int32, (CH, PIX), 1)
    third = []
    for c in range(NC):
        cs = slice(c * CH, (c + 1) * CH)
        for cp in second[c * (NS - 1):(c + 1) * (NS - 1)]:
            cp.wait_recv()

        def place(j, _):
            one = j < l1
            p = jnp.where(one, p1 + j, p2 + j - l1)
            q = p % CLS
            n1 = (l1 - (q - p1 + 256) % CLS + 7) // CLS
            r = jnp.where(one, j // CLS, n1 + (j - l1) // CLS)
            live = j < l1 + l2
            q = jnp.where(live, q, 0)
            r = jnp.where(live, r, 0)
            x = dbuf[c][q, r]
            gs[j, cs] = jnp.where(live, x, jnp.zeros_like(x))
            return 0

        lax.fori_loop(0, SLOTS, place, 0)
        if c == 0:
            for j in range(SLOTS, SLOTS + FD + 2):
                gs[j] = jnp.zeros((OG, PIX), jnp.bfloat16)

        for k in range(1, NH):
            h = (mh + k) % NH
            cp = pltpu.make_async_remote_copy(
                src_ref=gs.at[pl.ds(h * FD, FD + 2), chunks[c], :],
                dst_ref=ebuf.at[:, pl.ds(pl.multiple_of(mh * OG + c * CH, CH), CH), :],
                send_sem=s3.at[c, k], recv_sem=r3.at[c, k],
                device_id={"head": h}, device_id_type=MESH)
            third.append((h, cp))

            @pl.when(h < SLOTS // FD)
            def _(cp=cp):
                cp.start()

        def build(f, _):
            x = gs[f, cs]
            sh = shifts(x, lane)
            for d in range(3):
                keep = age(f) >= d
                at = pl.ds(pl.multiple_of((f - d + 2) * PIX, PIX), PIX)
                for ab in range(9):
                    v = sh[ab]
                    if d:
                        v = jnp.where(keep, v, jnp.zeros_like(v))
                    t = 9 * (2 - d) + ab
                    taps[(c * 27 + t) * CH:(c * 27 + t + 1) * CH, at] = v
            return 0

        lax.fori_loop(0, SLOTS + 2, build, 0, unroll=5)
    own3 = pltpu.make_async_copy(
        gs.at[pl.ds(mh * FD, FD + 2)],
        ebuf.at[:, pl.ds(pl.multiple_of(mh * OG, OG), OG), :], lo.at[0])
    own3.start()

    for cp in loads:
        cp.wait()
    part[...] = jnp.zeros_like(part)
    fourth = []
    for e, (lo_t, hi_t) in enumerate(CUTS):
        def mul(n, _):
            a4 = act_v[:, pl.ds(pl.multiple_of(n * 4 * PIX, 4 * PIX), 4 * PIX)]
            b4 = taps[lo_t:hi_t, pl.ds(pl.multiple_of((n * 4 + 2) * PIX, 2 * PIX), 4 * PIX)]
            part[:, lo_t:hi_t] += lax.dot_general(
                a4, b4, (((1,), (1,)), ((), ())), preferred_element_type=jnp.float32)
            return 0

        lax.fori_loop(0, SLOTS // 4, mul, 0)
        for k in list(range(1, NS)) + [0]:
            d = (ms + k) % NS
            psend[e][d] = (
                part[pl.ds(pl.multiple_of(d * 24, 8), 24), lo_t:hi_t] * SCALE
            ).astype(jnp.bfloat16)
            if k:
                cp = pltpu.make_async_remote_copy(
                    src_ref=psend[e].at[d], dst_ref=precv[e].at[ms],
                    send_sem=s4.at[e, k], recv_sem=r4.at[e, k],
                    device_id={"slab": d}, device_id_type=MESH)
                cp.start()
                fourth.append(cp)
        precv[e][ms] = psend[e][ms]

    own3.wait()
    for cp in wloads:
        cp.wait()
    lane384 = lax.broadcasted_iota(jnp.int32, (C, PIX), 1)

    def hbuild(f, _):
        sh = shifts(ebuf[f], lane384)
        at = pl.ds(pl.multiple_of(f * PIX, PIX), PIX)
        for ab in range(9):
            hbuf[ab * C:(ab + 1) * C, at] = sh[ab]
        return 0

    def grad(f, _):
        total = jnp.zeros((C, PIX), jnp.float32)
        for d in range(3):
            at = pl.ds(pl.multiple_of((f + d) * PIX, PIX), PIX)
            y = jnp.dot(w_v[2 - d], hbuf[:, at], preferred_element_type=jnp.float32)
            if d:
                y = jnp.where(age(mh * FD + f + d) >= d, y, 0.0)
            total += y
        total = total.astype(jnp.bfloat16)
        for h in range(NH):
            osend[f, h] = total[h * OG:(h + 1) * OG]
        for k in range(1, NH):
            out_copy(k, f).start()
        return 0

    def out_copy(k, f):
        h = (mh + k) % NH
        return pltpu.make_async_remote_copy(
            src_ref=osend.at[f, h], dst_ref=xbuf.at[mh * FD + f],
            send_sem=s5.at[k, f], recv_sem=r5.at[k, f],
            device_id={"head": h}, device_id_type=MESH)

    @pl.when(low)
    def _():
        for _, cp in third:
            cp.wait_recv()
        lax.fori_loop(0, FD + 2, hbuild, 0)
        lax.fori_loop(0, FD, grad, 0)
        xbuf[pl.ds(mh * FD, FD)] = osend[:, mh]

    for cp in fourth:
        cp.wait()
    sums = []
    for e in range(2):
        acc = precv[e][0].astype(jnp.float32)
        for k in range(1, NS):
            acc += precv[e][k].astype(jnp.float32)
        sums.append(acc.astype(jnp.bfloat16))
    for c in range(NC):
        for t in range(27):
            at = (c * 27 + t) * CH
            e = 1 if at >= CUTS[1][0] else 0
            at -= CUTS[e][0]
            dw[t, :, c * CH:(c + 1) * CH] = sums[e][:, at:at + CH]

    for cp in first + second:
        cp.wait_send()
    for h, cp in third:
        @pl.when(h < SLOTS // FD)
        def _(cp=cp):
            cp.wait_send()

    @pl.when(low)
    def _():
        for k in range(1, NH):
            for f in range(FD):
                out_copy(k, f).wait_send()

    for k in range(1, NH):
        @pl.when((mh - k + NH) % NH < SLOTS // FD)
        def _(k=k):
            for f in range(FD):
                out_copy(k, f).wait_recv()

    dx[...] = xbuf[pl.ds(0, SLOTS)]


def shards(act, w, g, clip_length, clip_slab_index, packed_clip_order):
    bf = jnp.bfloat16
    dma = pltpu.SemaphoreType.DMA
    anyspace = pl.BlockSpec(memory_space=pl.ANY)
    vmem = pl.BlockSpec(memory_space=pltpu.VMEM)
    dx, dw = pl.pallas_call(
        body,
        out_shape=(
            jax.ShapeDtypeStruct((SLOTS, OG, PIX), bf),
            jax.ShapeDtypeStruct((27, 24, OG), bf),
        ),
        in_specs=[pl.BlockSpec(memory_space=pltpu.SMEM)] * 3 + [anyspace, anyspace, anyspace],
        out_specs=(vmem, vmem),
        scratch_shapes=[
            pltpu.SMEM((3, CLIPS), jnp.int32),
            pltpu.SMEM((NS * 4,), jnp.int32),
            pltpu.SMEM((NS * PER,), jnp.int32),
            pltpu.VMEM((C, SLOTS * PIX), bf),
            pltpu.VMEM((3, C, 9 * C), bf),
            *[pltpu.VMEM((NS, 2, CH, 128), bf) for _ in range(NC)],
            pltpu.VMEM((NS, PER, OG, 128), bf),
            *[pltpu.VMEM((CLS, PER, CH, PIX), bf) for _ in range(NC)],
            pltpu.VMEM((SLOTS + FD + 2, OG, PIX), bf),
            pltpu.VMEM((27 * OG, (SLOTS + 4) * PIX), bf),
            pltpu.VMEM((C, 27 * OG), jnp.float32),
            *[pltpu.VMEM((NS, 24, CUTS[e][1] - CUTS[e][0]), bf) for e in (0, 1, 0, 1)],
            pltpu.VMEM((FD + 2, C, PIX), bf),
            pltpu.VMEM((9 * C, (FD + 2) * PIX), bf),
            pltpu.VMEM((FD, NH, OG, PIX), bf),
            pltpu.VMEM((NH * FD, OG, PIX), bf),
            dma((NC, NS)), dma((NC, NS)), dma((NC, NS)), dma((NC, NS)),
            dma((NC, NH)), dma((NC, NH)), dma((2, NS)), dma((2, NS)),
            dma((NH, FD)), dma((NH, FD)),
            dma((SLOTS,)), dma((27,)), dma((NC,)),
        ],
        compiler_params=pltpu.CompilerParams(
            collective_id=0, has_side_effects=True, vmem_limit_bytes=67043328),
    )(clip_length, clip_slab_index, packed_clip_order, g.reshape(2, 8, OG, PIX), act, w)
    return dx, dw


def solution(mesh):
    return jax.shard_map(
        shards,
        mesh=mesh,
        in_specs=(P("slab", None, None), P(), P("slab", "head", None), P(), P(), P()),
        out_specs=(P("slab", "head", None), P(None, "slab", "head")),
        check_vma=False,
    )
```

```python
import functools
import math

import jax
import jax.numpy as jnp
from jax import lax
from jax.experimental import pallas as pl
from jax.experimental.pallas import tpu as pltpu
from jax.sharding import PartitionSpec as P

MESH = pl.DeviceIdType.MESH
ROWS = 16
COLS = 16
PIX = ROWS * COLS
SLOTS = 28
C = 384
OG = 48
NS = 16
NH = 8
CLS = 8
PER = 5
FD = 4
NC = 3
CH = OG // NC
CLIPS = 32
CUTS = ((0, 1024), (1024, 27 * OG))
SCALE = 1.0 / math.sqrt(256 * PIX)


def clip_table(length, slab, order, pk, tab):
    def walk(k, at):
        c = order[k]
        n = length[c]
        pk[0, k] = slab[c]
        pk[1, k] = n
        pk[2, k] = at
        return at + n

    lax.fori_loop(0, CLIPS, walk, 0)

    def row(d, _):
        ka, kb = jnp.int32(0), jnp.int32(0)
        for k in range(CLIPS):
            hit = pk[0, k] == d
            kb = jnp.where(hit, ka, kb)
            ka = jnp.where(hit, k, ka)
        swap = order[ka] > order[kb]
        k1 = jnp.where(swap, kb, ka)
        k2 = jnp.where(swap, ka, kb)
        tab[d * 4] = pk[2, k1]
        tab[d * 4 + 1] = pk[1, k1]
        tab[d * 4 + 2] = pk[2, k2]
        tab[d * 4 + 3] = pk[1, k2]
        return 0

    lax.fori_loop(0, NS, row, 0)


def shifts(x, lane):
    row, col = lane // COLS, lane % COLS
    out = []
    for a in range(3):
        for b in range(3):
            dr, dc = 1 - a, 1 - b
            off = dr * COLS + dc
            if off == 0:
                out.append(x)
                continue
            moved = pltpu.roll(x, (-off) % PIX, 1)
            ok = (row + dr >= 0) & (row + dr < ROWS) & (col + dc >= 0) & (col + dc < COLS)
            out.append(jnp.where(ok, moved, jnp.zeros_like(moved)))
    return out


def body(
    length, slab, order, g, act, w, dx, dw,
    pk, tab, pick, act_v, w_v, rbuf0, rbuf1, rbuf2, qbuf, dbuf0, dbuf1, dbuf2, gs, taps, part, psend0, psend1, precv0, precv1, ebuf, hbuf, osend, xbuf,
    s1, r1, s2, r2, s3, r3, s4, r4, s5, r5, la, lw, lo,
):
    ms = lax.axis_index("slab")
    mh = lax.axis_index("head")

    loads = []
    for f in range(SLOTS):
        loads.append(pltpu.make_async_copy(
            act.at[f], act_v.at[:, pl.ds(f * PIX, PIX)], la.at[f]))
    wloads = []
    for t in range(27):
        wloads.append(pltpu.make_async_copy(
            w.at[t], w_v.at[t // 9, :, pl.ds((t % 9) * C, C)], lw.at[t]))
    for cp in loads + wloads:
        cp.start()

    barrier = pltpu.get_barrier_semaphore()
    for k in range(1, NS):
        pl.semaphore_signal(barrier, inc=1, device_id={"slab": (ms + k) % NS}, device_id_type=MESH)
    for k in range(1, NH):
        pl.semaphore_signal(barrier, inc=1, device_id={"head": (mh + k) % NH}, device_id_type=MESH)
    pl.semaphore_wait(barrier, NS - 1 + NH - 1)

    def piece(d, cs):
        return g.at[:, d // 2, cs, pl.ds(pl.multiple_of((d % 2) * 128, 128), 128)]

    psend, precv = (psend0, psend1), (precv0, precv1)
    rbuf, dbuf = (rbuf0, rbuf1, rbuf2), (dbuf0, dbuf1, dbuf2)
    chunks = [pl.ds(c * CH, CH) for c in range(NC)]
    own = []
    for c in range(NC):
        cp = pltpu.make_async_copy(piece(ms, chunks[c]), rbuf[c].at[ms], lo.at[c])
        cp.start()
        own.append(cp)
    first = []
    for c in range(NC):
        for k in range(1, NS):
            d = (ms + k) % NS
            cp = pltpu.make_async_remote_copy(
                src_ref=piece(d, chunks[c]), dst_ref=rbuf[c].at[ms],
                send_sem=s1.at[c, k], recv_sem=r1.at[c, k],
                device_id={"slab": d}, device_id_type=MESH)
            cp.start()
            first.append(cp)

    clip_table(length, slab, order, pk, tab)
    cls = ms // 2
    half = pl.ds(pl.multiple_of((ms % 2) * 128, 128), 128)

    def choose(d, _):
        p1, l1, p2 = tab[d * 4], tab[d * 4 + 1], tab[d * 4 + 2]
        o1 = (cls - p1 + 256) % CLS
        o2 = (cls - p2 + 256) % CLS
        n1 = (l1 - o1 + 7) // CLS
        for j in range(PER):
            i1 = (p1 + o1) // CLS + j
            i2 = (p2 + o2) // CLS + j - n1
            idx = jnp.where(j < n1, i1, i2)
            pick[d * PER + j] = jnp.minimum(jnp.maximum(idx, 0), 31)
        return 0

    lax.fori_loop(0, NS, choose, 0)
    for cp in own:
        cp.wait()
    second = []
    for c in range(NC):
        for cp in first[c * (NS - 1):(c + 1) * (NS - 1)]:
            cp.wait_recv()
        for k in list(range(1, NS)) + [0]:
            d = (ms + k) % NS
            for j in range(PER):
                idx = pick[d * PER + j]
                qbuf[d, j, c * CH:(c + 1) * CH] = rbuf[c][idx // 2, idx % 2]
            if k:
                cp = pltpu.make_async_remote_copy(
                    src_ref=qbuf.at[d, :, chunks[c], :],
                    dst_ref=dbuf[c].at[cls, :, :, half],
                    send_sem=s2.at[c, k], recv_sem=r2.at[c, k],
                    device_id={"slab": d}, device_id_type=MESH)
                cp.start()
                second.append(cp)
    own = []
    for c in range(NC):
        cp = pltpu.make_async_copy(
            qbuf.at[ms, :, chunks[c], :], dbuf[c].at[cls, :, :, half], lo.at[c])
        cp.start()
        own.append(cp)
    for cp in own:
        cp.wait()

    p1, l1, p2, l2 = tab[ms * 4], tab[ms * 4 + 1], tab[ms * 4 + 2], tab[ms * 4 + 3]

    def age(j):
        return jnp.where(j < l1, j, j - l1)

    low = mh < SLOTS // FD
    lane = lax.broadcasted_iota(jnp.int32, (CH, PIX), 1)
    third = []
    for c in range(NC):
        cs = slice(c * CH, (c + 1) * CH)
        for cp in second[c * (NS - 1):(c + 1) * (NS - 1)]:
            cp.wait_recv()

        def place(j, _):
            one = j < l1
            p = jnp.where(one, p1 + j, p2 + j - l1)
            q = p % CLS
            n1 = (l1 - (q - p1 + 256) % CLS + 7) // CLS
            r = jnp.where(one, j // CLS, n1 + (j - l1) // CLS)
            live = j < l1 + l2
            q = jnp.where(live, q, 0)
            r = jnp.where(live, r, 0)
            x = dbuf[c][q, r]
            gs[j, cs] = jnp.where(live, x, jnp.zeros_like(x))
            return 0

        lax.fori_loop(0, SLOTS, place, 0)
        if c == 0:
            for j in range(SLOTS, SLOTS + FD + 2):
                gs[j] = jnp.zeros((OG, PIX), jnp.bfloat16)

        for k in range(1, NH):
            h = (mh + k) % NH
            cp = pltpu.make_async_remote_copy(
                src_ref=gs.at[pl.ds(h * FD, FD + 2), chunks[c], :],
                dst_ref=ebuf.at[:, pl.ds(pl.multiple_of(mh * OG + c * CH, CH), CH), :],
                send_sem=s3.at[c, k], recv_sem=r3.at[c, k],
                device_id={"head": h}, device_id_type=MESH)
            third.append((h, cp))

            @pl.when(h < SLOTS // FD)
            def _(cp=cp):
                cp.start()

        def build(f, _):
            x = gs[f, cs]
            sh = shifts(x, lane)
            for d in range(3):
                keep = age(f) >= d
                at = pl.ds(pl.multiple_of((f - d + 2) * PIX, PIX), PIX)
                for ab in range(9):
                    v = sh[ab]
                    if d:
                        v = jnp.where(keep, v, jnp.zeros_like(v))
                    t = 9 * (2 - d) + ab
                    taps[(c * 27 + t) * CH:(c * 27 + t + 1) * CH, at] = v
            return 0

        lax.fori_loop(0, SLOTS + 2, build, 0, unroll=5)
    own3 = pltpu.make_async_copy(
        gs.at[pl.ds(mh * FD, FD + 2)],
        ebuf.at[:, pl.ds(pl.multiple_of(mh * OG, OG), OG), :], lo.at[0])
    own3.start()

    for cp in loads:
        cp.wait()
    part[...] = jnp.zeros_like(part)
    fourth = []
    for e, (lo_t, hi_t) in enumerate(CUTS):
        def mul(n, _):
            a4 = act_v[:, pl.ds(pl.multiple_of(n * 4 * PIX, 4 * PIX), 4 * PIX)]
            b4 = taps[lo_t:hi_t, pl.ds(pl.multiple_of((n * 4 + 2) * PIX, 2 * PIX), 4 * PIX)]
            part[:, lo_t:hi_t] += lax.dot_general(
                a4, b4, (((1,), (1,)), ((), ())), preferred_element_type=jnp.float32)
            return 0

        lax.fori_loop(0, SLOTS // 4, mul, 0)
        for k in list(range(1, NS)) + [0]:
            d = (ms + k) % NS
            psend[e][d] = (
                part[pl.ds(pl.multiple_of(d * 24, 8), 24), lo_t:hi_t] * SCALE
            ).astype(jnp.bfloat16)
            if k:
                cp = pltpu.make_async_remote_copy(
                    src_ref=psend[e].at[d], dst_ref=precv[e].at[ms],
                    send_sem=s4.at[e, k], recv_sem=r4.at[e, k],
                    device_id={"slab": d}, device_id_type=MESH)
                cp.start()
                fourth.append(cp)
        precv[e][ms] = psend[e][ms]

    own3.wait()
    for cp in wloads:
        cp.wait()
    lane384 = lax.broadcasted_iota(jnp.int32, (C, PIX), 1)

    def hbuild(f, _):
        sh = shifts(ebuf[f], lane384)
        at = pl.ds(pl.multiple_of(f * PIX, PIX), PIX)
        for ab in range(9):
            hbuf[ab * C:(ab + 1) * C, at] = sh[ab]
        return 0

    def grad(f, _):
        total = jnp.zeros((C, PIX), jnp.float32)
        for d in range(3):
            at = pl.ds(pl.multiple_of((f + d) * PIX, PIX), PIX)
            y = jnp.dot(w_v[2 - d], hbuf[:, at], preferred_element_type=jnp.float32)
            if d:
                y = jnp.where(age(mh * FD + f + d) >= d, y, 0.0)
            total += y
        total = total.astype(jnp.bfloat16)
        for h in range(NH):
            osend[f, h] = total[h * OG:(h + 1) * OG]
        for k in range(1, NH):
            out_copy(k, f).start()
        return 0

    def out_copy(k, f):
        h = (mh + k) % NH
        return pltpu.make_async_remote_copy(
            src_ref=osend.at[f, h], dst_ref=xbuf.at[mh * FD + f],
            send_sem=s5.at[k, f], recv_sem=r5.at[k, f],
            device_id={"head": h}, device_id_type=MESH)

    @pl.when(low)
    def _():
        for _, cp in third:
            cp.wait_recv()
        lax.fori_loop(0, FD + 2, hbuild, 0)
        lax.fori_loop(0, FD, grad, 0)
        xbuf[pl.ds(mh * FD, FD)] = osend[:, mh]

    for cp in fourth:
        cp.wait()
    sums = []
    for e in range(2):
        acc = precv[e][0].astype(jnp.float32)
        for k in range(1, NS):
            acc += precv[e][k].astype(jnp.float32)
        sums.append(acc.astype(jnp.bfloat16))
    for c in range(NC):
        for t in range(27):
            at = (c * 27 + t) * CH
            e = 1 if at >= CUTS[1][0] else 0
            at -= CUTS[e][0]
            dw[t, :, c * CH:(c + 1) * CH] = sums[e][:, at:at + CH]

    for cp in first + second:
        cp.wait_send()
    for h, cp in third:
        @pl.when(h < SLOTS // FD)
        def _(cp=cp):
            cp.wait_send()

    @pl.when(low)
    def _():
        for k in range(1, NH):
            for f in range(FD):
                out_copy(k, f).wait_send()

    for k in range(1, NH):
        @pl.when((mh - k + NH) % NH < SLOTS // FD)
        def _(k=k):
            for f in range(FD):
                out_copy(k, f).wait_recv()

    dx[...] = xbuf[pl.ds(0, SLOTS)]


def shards(act, w, g, clip_length, clip_slab_index, packed_clip_order):
    bf = jnp.bfloat16
    dma = pltpu.SemaphoreType.DMA
    anyspace = pl.BlockSpec(memory_space=pl.ANY)
    vmem = pl.BlockSpec(memory_space=pltpu.VMEM)
    dx, dw = pl.pallas_call(
        body,
        out_shape=(
            jax.ShapeDtypeStruct((SLOTS, OG, PIX), bf),
            jax.ShapeDtypeStruct((27, 24, OG), bf),
        ),
        in_specs=[pl.BlockSpec(memory_space=pltpu.SMEM)] * 3 + [anyspace, anyspace, anyspace],
        out_specs=(vmem, vmem),
        scratch_shapes=[
            pltpu.SMEM((3, CLIPS), jnp.int32),
            pltpu.SMEM((NS * 4,), jnp.int32),
            pltpu.SMEM((NS * PER,), jnp.int32),
            pltpu.VMEM((C, SLOTS * PIX), bf),
            pltpu.VMEM((3, C, 9 * C), bf),
            *[pltpu.VMEM((NS, 2, CH, 128), bf) for _ in range(NC)],
            pltpu.VMEM((NS, PER, OG, 128), bf),
            *[pltpu.VMEM((CLS, PER, CH, PIX), bf) for _ in range(NC)],
            pltpu.VMEM((SLOTS + FD + 2, OG, PIX), bf),
            pltpu.VMEM((27 * OG, (SLOTS + 4) * PIX), bf),
            pltpu.VMEM((C, 27 * OG), jnp.float32),
            *[pltpu.VMEM((NS, 24, CUTS[e][1] - CUTS[e][0]), bf) for e in (0, 1, 0, 1)],
            pltpu.VMEM((FD + 2, C, PIX), bf),
            pltpu.VMEM((9 * C, (FD + 2) * PIX), bf),
            pltpu.VMEM((FD, NH, OG, PIX), bf),
            pltpu.VMEM((NH * FD, OG, PIX), bf),
            dma((NC, NS)), dma((NC, NS)), dma((NC, NS)), dma((NC, NS)),
            dma((NC, NH)), dma((NC, NH)), dma((2, NS)), dma((2, NS)),
            dma((NH, FD)), dma((NH, FD)),
            dma((SLOTS,)), dma((27,)), dma((NC,)),
        ],
        compiler_params=pltpu.CompilerParams(
            collective_id=0, has_side_effects=True, vmem_limit_bytes=67043328),
    )(clip_length, clip_slab_index, packed_clip_order, g.reshape(2, 8, OG, PIX), act, w)
    return dx, dw


def solution(mesh):
    return jax.shard_map(
        shards,
        mesh=mesh,
        in_specs=(P("slab", None, None), P(), P("slab", "head", None), P(), P(), P()),
        out_specs=(P("slab", "head", None), P(None, "slab", "head")),
        check_vma=False,
    )
```
